256 devices in a mesh: dp: 32 (over y, x, core), tensor: 8 (over z).
Axes of the slice: x: 4, y: 4, z: 8, core: 2. Of those that a mesh axis runs over, the one named last changes fastest.
Arguments:
- old_master: float32 [8, 32, 1536, 128], P('tensor', 'dp'), may hold values from -0.25 to 0.25
- old_moment1: float32 [8, 32, 1536, 128], P('tensor', 'dp'), may hold values from -6 to 6
- old_moment2: float32 [8, 32, 1536, 128], P('tensor', 'dp'), may hold values from 0.1 to 1
- old_counts: int32 [32], replicated, may hold values from 1 to 1536, 32768 in all
- old_owner: int32 [32], replicated, may hold values from 0 to 31, each once
- inputs: bfloat16 [16384, 4096], P('dp', 'tensor'), may hold values from -6 to 6
- cotangent: bfloat16 [16384, 8192], P(('dp', 'tensor')), may hold values from -0.5 to 0.5
Outputs:
- new_master: float32 [4096, 8192], P('tensor', 'dp')
- new_moment1: float32 [4096, 8192], P('tensor', 'dp')
- new_moment2: float32 [4096, 8192], P('tensor', 'dp')
- input_grad: bfloat16 [16384, 4096], P('dp', 'tensor')
The draws below stay inside these ranges and needn't reach their ends.
Inputs may be any that keep to these rules, and one draw needn't show every extreme that they name: `old_counts`: the old ranges are contiguous in rank order and cover all 32768 units; some rank holds exactly 1536. `old_owner`: each dp index holds exactly one old rank's range.
All inputs are finite; a program needn't handle non-finite values.
Results may differ from the reference program's by a relative error of at most 0.0049.
Values may be sent and summed in bfloat16 or wider, within the bound.
A program may use at most 128 MiB of HBM per device.

```python
import math
import jax
import jax.numpy as jnp
import numpy as np
from jax import lax

D = 8192
UNIT = 128
TOKENS = 16384
HD = 4096
UNITS = 32768
MOST = 1536
N_DP = 32
N_TENSOR = 8


def raised(values, own_key, source, target, shards_of, factor):
    owner, partner = [(jnp.arange(values.shape[axis_at]) // (values.shape[axis_at] // shards_of)).reshape([-1 if axis == axis_at else 1 for axis in range(values.ndim)]) for axis_at in (source, target)]
    chosen = jax.random.permutation(own_key, shards_of)[partner]
    strong = (owner == chosen) | (owner == (partner + shards_of // 2) % shards_of)
    return jnp.where(strong, factor * values, values)


def block_scale(rng, shape, split, least, high):
    level = 1.0
    for position, parts in split:
        heights = jax.random.uniform(jax.random.fold_in(jax.random.fold_in(rng, 6), position), (parts,), jnp.float32, least / len(split), high / len(split))
        level = level * jnp.repeat(jnp.exp(heights), shape[position] // parts).reshape((-1,) + (1,) * (len(shape) - 1 - position))
    return level


def split_up(number_of, total, reach, skew):
    portions = [(1 << 20) // math.isqrt(standing ** skew) + 1 for standing in range(2, number_of + 1)]
    spare, counts = total - reach - (number_of - 1), [1] * (number_of - 1)
    while spare > 0:
        free = [i for i in range(number_of - 1) if counts[i] < reach]
        pool, left = sum([portions[i] for i in free]), spare
        for i in free:
            more = min(reach - counts[i], max(1, left * portions[i] // pool), spare)
            counts[i] = counts[i] + more
            spare = spare - more
    return np.array([reach] + counts)


def ragged_sizes(rng, number_of, total, bound, skew):
    if number_of == 2:
        one = jax.random.randint(rng, (), max(1, total - bound), min(bound, total - 1) + 1)
        return jnp.stack([one, total - one])
    sizes = jnp.asarray(split_up(number_of, total, bound, skew), jnp.int32)
    couples = (number_of - 1) // 2
    giver, receiver = sizes[1:1 + 2 * couples:2], sizes[2:2 + 2 * couples:2]
    slack = jnp.minimum(giver - 1, bound - receiver)
    shifted = jax.random.randint(jax.random.fold_in(rng, 1), (couples,), 0, 1 << 20) % (slack + 1)
    sizes = sizes.at[1:1 + 2 * couples:2].set(giver - shifted).at[2:2 + 2 * couples:2].set(receiver + shifted)
    return sizes[jax.random.permutation(jax.random.fold_in(rng, 2), number_of)]


def scatter_about(stream_key, shape, width, limit, shards=(), kind=jnp.bfloat16):
    loudness = block_scale(stream_key, shape, shards, -0.22, 0.18) if shards else 1.0
    values = jax.random.normal(stream_key, shape, jnp.float32) * width * loudness
    return jnp.minimum(jnp.maximum(values, -limit), limit).astype(kind)


def heavy_noise(key, shape, deviation, most, split, heavy, kind=jnp.bfloat16):
    entries = deviation * jax.random.normal(key, shape, jnp.float32)
    if split:
        entries = entries * block_scale(key, shape, split, -0.22, 0.18)
    return jnp.clip(raised(entries, jax.random.fold_in(key, 3), *heavy), -most, most).astype(kind)


def setup_inputs(seed: int = 0) -> dict:
    splits = jax.random.split(jax.random.key(seed), 8)
    old_master = scatter_about(splits[0], (N_TENSOR, N_DP, MOST, UNIT), (HD ** -0.5), 0.25, ((0, 8), (1, 32)), jnp.float32)
    old_moment1 = scatter_about(splits[1], (N_TENSOR, N_DP, MOST, UNIT), 0.5, 6.0, ((0, 8), (1, 32)), jnp.float32)
    old_moment2 = jnp.clip(jnp.exp(math.log(1.0) - 2.3025851 * jax.random.uniform(splits[2], (N_TENSOR, N_DP, MOST, UNIT), jnp.float32) ** block_scale(splits[2], (N_TENSOR, N_DP, MOST, UNIT), ((0, 8), (1, 32)), -0.2, 0.2)), 0.1, 1.0)
    old_counts = ragged_sizes(splits[3], N_DP, UNITS, MOST, 2).astype(jnp.int32)
    old_owner = jax.random.permutation(splits[4], N_DP).astype(jnp.int32)
    inputs = scatter_about(splits[5], (TOKENS, HD), 1.0, 6.0, ((0, 32), (1, 8)))
    cotangent = heavy_noise(splits[6], (TOKENS, D), (TOKENS ** -0.5), 0.5, ((0, 256),), (0, 1, 256, 6.0))
    return {"old_master": old_master, "old_moment1": old_moment1, "old_moment2": old_moment2, "old_counts": old_counts, "old_owner": old_owner, "inputs": inputs, "cotangent": cotangent}


learn_rate = 0.003
beta_one = 0.9
beta_two = 0.95
epsilon = 1e-08
weight_decay = 0.1

def relay(old_state, starts, ends, old_owner):
    tensor_count, dp_count, capacity_old, unit_len = old_state.shape
    unit_ids = jnp.arange(UNITS, dtype=jnp.int32)
    owner_rank = lax.optimization_barrier(jnp.sum((ends[None, :] <= unit_ids[:, None]).astype(jnp.int32), axis=1)).astype(jnp.int32)
    start_of = jnp.take(starts, owner_rank).astype(jnp.int32)
    holder = jnp.take(old_owner, owner_rank).astype(jnp.int32)
    flat_index = (holder * capacity_old + unit_ids - start_of).astype(jnp.int32)
    flat_state = old_state.reshape(tensor_count, dp_count * capacity_old, unit_len)
    picked = jnp.take(flat_state, flat_index, axis=1)
    return picked.reshape(HD, D)

def reference(old_master, old_moment1, old_moment2, old_counts, old_owner, inputs, cotangent):
    ends = jnp.cumsum(old_counts).astype(jnp.int32)
    starts = (ends - old_counts).astype(jnp.int32)
    master = relay(old_master, starts, ends, old_owner)
    moment1 = relay(old_moment1, starts, ends, old_owner)
    moment2 = relay(old_moment2, starts, ends, old_owner)
    weight = master.astype(jnp.bfloat16)
    input_grad = lax.dot_general(cotangent, weight, (((1,), (1,)), ((), ())), preferred_element_type=jnp.float32).astype(jnp.bfloat16)
    grad = lax.dot_general(inputs, cotangent, (((0,), (0,)), ((), ())), preferred_element_type=jnp.float32)
    new_moment1 = beta_one * moment1 + (1.0 - beta_one) * grad
    new_moment2 = beta_two * moment2 + (1.0 - beta_two) * grad * grad
    new_master = master - learn_rate * (new_moment1 / (jnp.sqrt(new_moment2) + epsilon) + weight_decay * master)
    return (new_master, new_moment1, new_moment2, input_grad)
```

```python
import jax
import jax.numpy as jnp
from jax import lax
from jax.sharding import PartitionSpec as P

learn_rate = 0.003
beta_one = 0.9
beta_two = 0.95
epsilon = 1e-08
weight_decay = 0.1


def local(old_master, old_moment1, old_moment2, old_counts, old_owner, inputs, cotangent):
    dp_count = lax.axis_size("dp")
    my_index = lax.axis_index("dp")
    capacity_old = old_master.shape[2]
    unit_len = old_master.shape[3]
    rows_here = inputs.shape[1]
    width = cotangent.shape[1]
    per_row = width // unit_len
    per_dest = per_row // dp_count
    slots = -(-capacity_old // per_row)
    rank_ids = jnp.arange(dp_count, dtype=jnp.int32)
    ends = jnp.cumsum(old_counts)
    starts = ends - old_counts
    my_start = jnp.sum(jnp.where(old_owner == my_index, starts, 0))
    state = jnp.concatenate(
        [
            part.reshape(capacity_old, unit_len).astype(jnp.bfloat16)
            for part in (old_master, old_moment1, old_moment2)
        ],
        axis=1,
    )
    columns = jnp.arange(per_row, dtype=jnp.int32)[:, None]
    steps = jnp.arange(slots, dtype=jnp.int32)[None, :]
    local_ids = (columns - my_start) % per_row + per_row * steps
    local_ids = jnp.minimum(local_ids, capacity_old - 1).reshape(-1)
    packed = jnp.take(state, local_ids, axis=0).reshape(dp_count, per_dest * slots, 3 * unit_len)
    got = lax.all_to_all(packed, "dp", split_axis=0, concat_axis=0, tiled=True)
    got = got.reshape(dp_count * per_dest * slots, 3 * unit_len)

    place_ids = jnp.arange(rows_here * per_dest, dtype=jnp.int32)
    column = place_ids % per_dest
    unit_ids = per_row * (place_ids // per_dest) + per_dest * my_index + column
    owner_rank = jnp.sum((ends[None, :] <= unit_ids[:, None]).astype(jnp.int32), axis=1)
    matches = rank_ids[None, :] == owner_rank[:, None]
    start_of = jnp.sum(jnp.where(matches, starts[None, :], 0), axis=1)
    holder = jnp.sum(jnp.where(matches, old_owner[None, :], 0), axis=1)
    step_of = (unit_ids - start_of) // per_row
    flat_index = (holder * per_dest + column) * slots + step_of
    placed = jnp.take(got, flat_index, axis=0).reshape(rows_here, per_dest, 3, unit_len)
    weight = placed[:, :, 0].reshape(rows_here, per_dest * unit_len)
    master = weight.astype(jnp.float32)
    moment1 = placed[:, :, 1].reshape(rows_here, per_dest * unit_len).astype(jnp.float32)
    moment2 = placed[:, :, 2].reshape(rows_here, per_dest * unit_len).astype(jnp.float32)
    needed = lax.all_gather(cotangent, "tensor", axis=0, tiled=True)
    input_grad = lax.dot_general(
        needed,
        lax.all_gather(weight, "dp", axis=1, tiled=True),
        (((1,), (1,)), ((), ())),
        preferred_element_type=jnp.float32,
    )
    partial = lax.dot_general(
        needed, inputs, (((0,), (0,)), ((), ())), preferred_element_type=jnp.float32
    ).astype(jnp.bfloat16)
    grad = lax.psum_scatter(partial, "dp", scatter_dimension=0, tiled=True).T.astype(jnp.float32)
    new_moment1 = beta_one * moment1 + (1.0 - beta_one) * grad
    new_moment2 = beta_two * moment2 + (1.0 - beta_two) * grad * grad
    new_master = master - learn_rate * (
        new_moment1 / (jnp.sqrt(new_moment2) + epsilon) + weight_decay * master
    )
    return (new_master, new_moment1, new_moment2, input_grad.astype(jnp.bfloat16))


def solution(mesh):
    placed = (
        P("tensor", "dp", None, None),
        P("tensor", "dp", None, None),
        P("tensor", "dp", None, None),
        P(),
        P(),
        P("dp", "tensor"),
        P(("dp", "tensor"), None),
    )
    return jax.shard_map(
        local,
        mesh=mesh,
        in_specs=placed,
        out_specs=(P("tensor", "dp"), P("tensor", "dp"), P("tensor", "dp"), P("dp", "tensor")),
        check_vma=False,
    )
```

```python
import jax
import jax.numpy as jnp
import numpy as np
from jax import lax
from jax.experimental import pallas as pl
from jax.experimental.pallas import tpu as pltpu
from jax.sharding import PartitionSpec as P

learn_rate = 0.003
beta_one = 0.9
beta_two = 0.95
epsilon = 1e-08
weight_decay = 0.1

MESH = pl.DeviceIdType.MESH
NX, NY, NC, NZ = 4, 4, 2, 8
NDP = NX * NY * NC
UNIT = 128
CHUNKS = 8
PER_ROW = 64
SLOTS = 24
TOK = 512
FEAT = 512
OWN = TOK // NZ
HALF_D = NX * UNIT


def when(cond):
    if isinstance(cond, (bool, np.bool_)):
        return (lambda f: f()) if cond else (lambda f: None)
    return pl.when(cond)


def both(*conds):
    out = True
    for cond in conds:
        out = jnp.logical_and(out, cond)
    return out


def kernel(
    wanted_rows, packed, x_hbm, cot,
    grad_out, master_out, moment1_out, moment2_out, ig,
    x_in, xt, g, wf, send, got, pair_s, pair_r, kept, xs, xr, kept_x, ys, yr,
    load_sem, own_sem, up_s, up_r, dn_s, dn_r, a2a_s, a2a_r,
    wx_s, wx_r, wy_s, wy_r, wp_s, wp_r, pr_s, pr_r, x_s, x_r, y_s, y_r,
):
    me = lax.axis_index("dp")
    z = lax.axis_index("tensor")
    c = me % NC
    x = (me // NC) % NX
    y = me // (NC * NX)
    up_dev = {"tensor": (z + 1) % NZ}
    dn_dev = {"tensor": (z + NZ - 1) % NZ}
    partner = {"dp": me + 1 - 2 * c}

    def dp_at(yy, xx, cc):
        return {"dp": (yy * NX + xx) * NC + cc}

    def remote(src, dst, ss, rs, dev):
        return pltpu.make_async_remote_copy(
            src_ref=src, dst_ref=dst, send_sem=ss, recv_sem=rs, device_id=dev, device_id_type=MESH
        )

    def row_of(s):
        return (y + s // 2 + 1) % NY

    def at(s):
        return row_of(s) * 2 + s % 2

    loads = [
        pltpu.make_async_copy(packed, send, load_sem.at[0]),
        pltpu.make_async_copy(x_hbm, x_in, load_sem.at[1]),
    ]

    def own(s, o):
        cc, xx = o // NX, o % NX
        j = (row_of(s) * NX + xx) * NC + cc
        col = pl.multiple_of(j * (2 * UNIT) + (s % 2) * UNIT, UNIT)
        return pltpu.make_async_copy(
            cot.at[:, pl.ds(col, UNIT)], g.at[at(s), z, o], own_sem.at[s, o]
        )

    def load_own(i, carry):
        own(i // 8, i % 8).start()
        return carry

    lax.fori_loop(0, 16, load_own, 0)
    for load in loads:
        load.start()
    lax.fori_loop(16, CHUNKS * 8, load_own, 0)

    barrier = pltpu.get_barrier_semaphore()

    def greet(d, carry):
        pl.semaphore_signal(barrier, inc=1, device_id={"dp": (me + d) % NDP}, device_id_type=MESH)
        return carry

    pl.semaphore_signal(barrier, inc=1, device_id=up_dev, device_id_type=MESH)
    pl.semaphore_signal(barrier, inc=1, device_id=dn_dev, device_id_type=MESH)
    lax.fori_loop(1, NDP, greet, 0)
    pl.semaphore_wait(barrier, NDP + 1)

    def z_up(s, h, back=0):
        blk = g.at[at(s), (z - (h - 1) - back + NZ) % NZ]
        return remote(blk, blk, up_s.at[s, h - 1], up_r.at[s, h - 1], up_dev)

    def z_dn(s, h, back=0):
        blk = g.at[at(s), (z + (h - 1) + back) % NZ]
        return remote(blk, blk, dn_s.at[s, h - 1], dn_r.at[s, h - 1], dn_dev)

    def z_own(s):
        for o in range(8):
            own(s, o).wait()
        z_up(s, 1).start()
        z_dn(s, 1).start()

    z_own(0)
    z_own(1)

    for load in loads:
        load.wait()
    got[me] = send[me]

    def a2a(d, source=None):
        j = (me + d) % NDP
        source = me if source is None else source
        return remote(send.at[j], got.at[source], a2a_s.at[d - 1], a2a_r.at[d - 1], {"dp": j})

    def a2a_start(d, carry):
        a2a(d).start()
        return carry

    lax.fori_loop(1, NDP, a2a_start, 0)
    xt[...] = x_in[...].astype(jnp.float32).T.astype(jnp.bfloat16)

    mine_o = c * NX + x

    def w_x(d, back=0):
        blk = wf.at[y, c * NX + (x + NX - back) % NX]
        return remote(blk, blk, wx_s.at[d - 1], wx_r.at[d - 1], dp_at(y, (x + d) % NX, c))

    def w_y(d, back=0):
        blk = wf.at[(y + NY - back) % NY, pl.ds(c * NX, NX)]
        return remote(blk, blk, wy_s.at[d - 1], wy_r.at[d - 1], dp_at((y + d) % NY, x, c))

    def w_pair(d, cc=None):
        cc = c if cc is None else cc
        blk = wf.at[(y + NY - d) % NY, pl.ds(cc * NX, NX)]
        return remote(blk, blk, wp_s.at[d], wp_r.at[d], partner)

    def assemble():
        def arrived(d, carry):
            a2a(d, (me + NDP - d) % NDP).wait_recv()
            return carry

        lax.fori_loop(1, NDP, arrived, 0)
        units = got[...].reshape(NDP * 2 * SLOTS, 3 * UNIT)
        for e in range(2):
            wanted = wanted_rows[e : e + 1, :]
            lanes = slice(e * UNIT, (e + 1) * UNIT)
            for base in range(0, FEAT, 128):
                ids = lax.broadcasted_iota(jnp.int32, (128, NDP * 2 * SLOTS), 0) + base
                pick = jnp.where(ids == wanted, 1.0, 0.0).astype(jnp.bfloat16)
                out = jnp.dot(pick, units, preferred_element_type=jnp.float32)
                here = slice(base, base + 128)
                wf[y, mine_o, e, here, :] = out[:, :UNIT].astype(jnp.bfloat16)
                master_out[here, lanes] = out[:, :UNIT]
                moment1_out[here, lanes] = out[:, UNIT : 2 * UNIT]
                moment2_out[here, lanes] = out[:, 2 * UNIT :]
        for d in range(1, NX):
            w_x(d).start()

    def weights_y():
        for d in range(1, NX):
            w_x(d, d).wait_recv()
        for d in range(1, NY):
            w_y(d).start()
        w_pair(0).start()

    def weights_pair():
        for d in range(1, NY):
            w_y(d, d).wait_recv()
            w_pair(d).start()

    def pair(s):
        return remote(pair_s.at[s], pair_r.at[s], pr_s.at[s], pr_r.at[s], partner)

    def along_x(s, d):
        xx = (x + d) % NX
        return remote(
            xs.at[s, xx], xr.at[s, d - 1], x_s.at[s, d - 1], x_r.at[s, d - 1], dp_at(y, xx, c)
        )

    def along_y(s):
        return remote(ys.at[s], yr.at[s], y_s.at[s], y_r.at[s], dp_at(row_of(s), x, c))

    def stage_c(s):
        for d in range(1, NX):
            along_x(s, d).wait_recv()
        total = kept_x[...]
        for d in range(NX - 1):
            total += xr[s, d].astype(jnp.float32)

        @when(s < 6)
        def _():
            ys[s] = total.astype(jnp.bfloat16)
            along_y(s).start()

        @when(s == 6)
        def _():
            grad_out[:, :UNIT] = total

        @when(s == 7)
        def _():
            grad_out[:, UNIT:] = total

    def stage_b(s):
        pair(s).wait_recv()
        for d in range(1, NX):
            xx = (x + d) % NX
            lanes = pl.ds(pl.multiple_of(xx * UNIT, UNIT), UNIT)
            xs[s, xx] = (kept[:, lanes] + pair_r[s, :, lanes].astype(jnp.float32)).astype(jnp.bfloat16)
            along_x(s, d).start()
        lanes = pl.ds(pl.multiple_of(x * UNIT, UNIT), UNIT)
        kept_x[...] = kept[:, lanes] + pair_r[s, :, lanes].astype(jnp.float32)

    def stage_a(s):
        @when(s % 2 == 0)
        def _():
            z_up(s, 4, 1).wait_recv()
            z_dn(s, 3, 1).wait_recv()

        @when(s % 2 == 1)
        def _():
            z_up(s, 3, 1).wait_recv()
            z_dn(s, 4, 1).wait_recv()

        def product(half):
            parts = [g[at(s), :, half * NX + i].reshape(TOK, UNIT) for i in range(NX)]
            block = jnp.concatenate(parts, axis=1)
            return jnp.dot(xt[...], block, preferred_element_type=jnp.float32)

        pair_s[s] = product(1 - c).astype(jnp.bfloat16)
        pair(s).start()
        kept[...] = product(c)

    def input_grad(s):
        rows = jnp.concatenate([g[at(s), :, o].reshape(TOK, UNIT) for o in range(8)], axis=1)
        weights = jnp.concatenate([wf[row_of(s), o, s % 2] for o in range(8)], axis=1)
        more = lax.dot_general(
            rows, weights, (((1,), (1,)), ((), ())), preferred_element_type=jnp.float32
        )

        @when(s == 0)
        def _():
            ig[...] = more

        @when(s > 0)
        def _():
            ig[...] += more

    def wave(w, carry):
        for h in (2, 3, 4):
            s = w - (h - 1)
            up_ok = both(s >= 0, s < CHUNKS)
            dn_ok = up_ok
            if h == 4:
                up_ok, dn_ok = both(up_ok, s % 2 == 0), both(dn_ok, s % 2 == 1)

            @when(up_ok)
            def _(s=s, h=h):
                z_up(s, h - 1, 1).wait_recv()
                z_up(s, h).start()

            @when(dn_ok)
            def _(s=s, h=h):
                z_dn(s, h - 1, 1).wait_recv()
                z_dn(s, h).start()

        @when(w + 1 < CHUNKS)
        def _():
            z_own(w + 1)

        @when(both(w >= 6, w < 14))
        def _():
            stage_c(w - 6)

        @when(both(w >= 5, w < 13))
        def _():
            stage_b(w - 5)

        @when(both(w >= 4, w < 12))
        def _():
            stage_a(w - 4)

        when(w == 2)(assemble)
        when(w == 4)(weights_y)
        when(w == 7)(weights_pair)

        @when(w == 8)
        def _():
            for d in range(NY):
                w_pair(d, 1 - c).wait_recv()

        @when(both(w >= 8, w < 12))
        def _():
            input_grad(2 * (w - 8))
            input_grad(2 * (w - 8) + 1)

        return carry

    lax.fori_loop(1, 14, wave, 0)

    for e in range(2):
        lanes = slice(e * UNIT, (e + 1) * UNIT)
        total = grad_out[:, lanes]
        for k in range(NY - 1):
            along_y(2 * k + e).wait_recv()
            total += yr[2 * k + e].astype(jnp.float32)
        grad_out[:, lanes] = total

    def sent_a2a(d, carry):
        a2a(d).wait_send()
        return carry

    lax.fori_loop(1, NDP, sent_a2a, 0)

    def sent(s, carry):
        for h in (1, 2, 3):
            z_up(s, h).wait_send()
            z_dn(s, h).wait_send()

        @when(s % 2 == 0)
        def _():
            z_up(s, 4).wait_send()

        @when(s % 2 == 1)
        def _():
            z_dn(s, 4).wait_send()

        pair(s).wait_send()
        for d in range(1, NX):
            along_x(s, d).wait_send()

        @when(s < 6)
        def _():
            along_y(s).wait_send()

        return carry

    lax.fori_loop(0, CHUNKS, sent, 0)
    for d in range(1, NX):
        w_x(d).wait_send()
    for d in range(1, NY):
        w_y(d).wait_send()
    for d in range(NY):
        w_pair(d).wait_send()


def old_places(counts, owners, me):
    index = jnp.arange(NDP, dtype=jnp.int32)
    starts = jnp.sum(jnp.where(index[None, :] < index[:, None], counts[None, :], 0), axis=1)
    holds = owners[None, :] == index[:, None]
    first = jnp.sum(jnp.where(holds, starts[None, :], 0), axis=1)
    last = first + jnp.sum(jnp.where(holds, counts[None, :], 0), axis=1)
    my_start = jnp.sum(jnp.where(owners == me, starts, 0))
    lane = np.arange(NDP * 2 * SLOTS)
    column = ((lane % (2 * SLOTS)) // SLOTS).astype(np.int32)
    step = ((lane % SLOTS) * PER_ROW).astype(np.int32)
    first = jnp.broadcast_to(first[:, None], (NDP, 2 * SLOTS)).reshape(-1)
    last = jnp.broadcast_to(last[:, None], (NDP, 2 * SLOTS)).reshape(-1)
    unit = first + ((2 * me + column - first) & (PER_ROW - 1)) + step
    row = jnp.where(unit < last, unit >> 6, -1)
    return my_start, jnp.stack([jnp.where(column == e, row, -1) for e in range(2)])


def local(old_master, old_moment1, old_moment2, old_counts, old_owner, inputs, cotangent):
    bf, f32 = jnp.bfloat16, jnp.float32
    dma = pltpu.SemaphoreType.DMA
    vmem = pl.BlockSpec(memory_space=pltpu.VMEM)
    anywhere = pl.BlockSpec(memory_space=pl.ANY)
    my_start, wanted_rows = old_places(old_counts, old_owner, lax.axis_index("dp"))

    def by_column(a):
        a = a.reshape(SLOTS, PER_ROW, UNIT).transpose(1, 0, 2)
        a = lax.dynamic_slice_in_dim(
            jnp.concatenate([a, a], axis=0), (-my_start) & (PER_ROW - 1), PER_ROW, axis=0
        )
        return a.reshape(NDP, 2 * SLOTS, UNIT)

    packed = jnp.concatenate(
        [by_column(a) for a in (old_master, old_moment1, old_moment2)], axis=2
    ).astype(bf)
    owned = jax.ShapeDtypeStruct((FEAT, 2 * UNIT), f32)
    grad, master, moment1, moment2, input_grad = pl.pallas_call(
        kernel,
        out_shape=(owned, owned, owned, owned, jax.ShapeDtypeStruct((TOK, FEAT), f32)),
        in_specs=[vmem] + [anywhere] * 3,
        out_specs=[vmem] * 5,
        scratch_shapes=[
            pltpu.VMEM((TOK, FEAT), bf),
            pltpu.VMEM((FEAT, TOK), bf),
            pltpu.VMEM((CHUNKS, NZ, NC * NX, OWN, UNIT), bf),
            pltpu.VMEM((NY, NC * NX, 2, FEAT, UNIT), bf),
            pltpu.VMEM((NDP, 2 * SLOTS, 3 * UNIT), bf),
            pltpu.VMEM((NDP, 2 * SLOTS, 3 * UNIT), bf),
            pltpu.VMEM((CHUNKS, FEAT, HALF_D), bf),
            pltpu.VMEM((CHUNKS, FEAT, HALF_D), bf),
            pltpu.VMEM((FEAT, HALF_D), f32),
            pltpu.VMEM((CHUNKS, NX, FEAT, UNIT), bf),
            pltpu.VMEM((CHUNKS, NX - 1, FEAT, UNIT), bf),
            pltpu.VMEM((FEAT, UNIT), f32),
            pltpu.VMEM((6, FEAT, UNIT), bf),
            pltpu.VMEM((6, FEAT, UNIT), bf),
            dma((2,)),
            dma((CHUNKS, 8)),
            dma((CHUNKS, 4)),
            dma((CHUNKS, 4)),
            dma((CHUNKS, 4)),
            dma((CHUNKS, 4)),
            dma((NDP - 1,)),
            dma((NDP - 1,)),
            dma((NX - 1,)),
            dma((NX - 1,)),
            dma((NY - 1,)),
            dma((NY - 1,)),
            dma((NY,)),
            dma((NY,)),
            dma((CHUNKS,)),
            dma((CHUNKS,)),
            dma((CHUNKS, NX - 1)),
            dma((CHUNKS, NX - 1)),
            dma((6,)),
            dma((6,)),
        ],
        compiler_params=pltpu.CompilerParams(
            collective_id=0, has_side_effects=True, vmem_limit_bytes=62 * 1024 * 1024
        ),
        name="relay_backward",
    )(wanted_rows, packed, inputs, cotangent)
    new_moment1 = beta_one * moment1 + (1.0 - beta_one) * grad
    new_moment2 = beta_two * moment2 + (1.0 - beta_two) * grad * grad
    new_master = master - learn_rate * (
        new_moment1 / (jnp.sqrt(new_moment2) + epsilon) + weight_decay * master
    )
    return (new_master, new_moment1, new_moment2, input_grad.astype(bf))


def solution(mesh):
    placed = (
        P("tensor", "dp", None, None),
        P("tensor", "dp", None, None),
        P("tensor", "dp", None, None),
        P(),
        P(),
        P("dp", "tensor"),
        P(("dp", "tensor"), None),
    )
    return jax.shard_map(
        local,
        mesh=mesh,
        in_specs=placed,
        out_specs=(P("tensor", "dp"), P("tensor", "dp"), P("tensor", "dp"), P("dp", "tensor")),
        check_vma=False,
    )
```

```python
import jax
import jax.numpy as jnp
import numpy as np
from jax import lax
from jax.experimental import pallas as pl
from jax.experimental.pallas import tpu as pltpu
from jax.sharding import PartitionSpec as P

learn_rate = 0.003
beta_one = 0.9
beta_two = 0.95
epsilon = 1e-08
weight_decay = 0.1

MESH = pl.DeviceIdType.MESH
NX, NY, NC, NZ = 4, 4, 2, 8
NDP = NX * NY * NC
UNIT = 128
CHUNKS = 8
PER_ROW = 64
SLOTS = 24
TOK = 512
FEAT = 512
OWN = TOK // NZ
HALF_D = NX * UNIT


def when(cond):
    if isinstance(cond, (bool, np.bool_)):
        return (lambda f: f()) if cond else (lambda f: None)
    return pl.when(cond)


def both(*conds):
    out = True
    for cond in conds:
        out = jnp.logical_and(out, cond)
    return out


def kernel(
    wanted_rows, packed, x_hbm, cot,
    grad_out, master_out, moment1_out, moment2_out, ig,
    x_in, xt, g, wf, send, got, pair_s, pair_r, kept, xs, xr, kept_x, ys, yr,
    load_sem, own_sem, up_s, up_r, dn_s, dn_r, a2a_s, a2a_r,
    wx_s, wx_r, wy_s, wy_r, wp_s, wp_r, pr_s, pr_r, x_s, x_r, y_s, y_r,
):
    me = lax.axis_index("dp")
    z = lax.axis_index("tensor")
    c = me % NC
    x = (me // NC) % NX
    y = me // (NC * NX)
    up_dev = {"tensor": (z + 1) % NZ}
    dn_dev = {"tensor": (z + NZ - 1) % NZ}
    partner = {"dp": me + 1 - 2 * c}

    def dp_at(yy, xx, cc):
        return {"dp": (yy * NX + xx) * NC + cc}

    def remote(src, dst, ss, rs, dev):
        return pltpu.make_async_remote_copy(
            src_ref=src, dst_ref=dst, send_sem=ss, recv_sem=rs, device_id=dev, device_id_type=MESH
        )

    def row_of(s):
        return (y + s // 2 + 1) % NY

    def at(s):
        return row_of(s) * 2 + s % 2

    loads = [
        pltpu.make_async_copy(packed, send, load_sem.at[0]),
        pltpu.make_async_copy(x_hbm, x_in, load_sem.at[1]),
    ]

    def own(s, o):
        cc, xx = o // NX, o % NX
        j = (row_of(s) * NX + xx) * NC + cc
        col = pl.multiple_of(j * (2 * UNIT) + (s % 2) * UNIT, UNIT)
        return pltpu.make_async_copy(
            cot.at[:, pl.ds(col, UNIT)], g.at[at(s), z, o], own_sem.at[s, o]
        )

    def load_own(i, carry):
        own(i // 8, i % 8).start()
        return carry

    lax.fori_loop(0, 16, load_own, 0)
    for load in loads:
        load.start()
    lax.fori_loop(16, CHUNKS * 8, load_own, 0)

    barrier = pltpu.get_barrier_semaphore()

    def greet(d, carry):
        pl.semaphore_signal(barrier, inc=1, device_id={"dp": (me + d) % NDP}, device_id_type=MESH)
        return carry

    pl.semaphore_signal(barrier, inc=1, device_id=up_dev, device_id_type=MESH)
    pl.semaphore_signal(barrier, inc=1, device_id=dn_dev, device_id_type=MESH)
    lax.fori_loop(1, NDP, greet, 0)
    pl.semaphore_wait(barrier, NDP + 1)

    def z_up(s, h, back=0):
        blk = g.at[at(s), (z - (h - 1) - back + NZ) % NZ]
        return remote(blk, blk, up_s.at[s, h - 1], up_r.at[s, h - 1], up_dev)

    def z_dn(s, h, back=0):
        blk = g.at[at(s), (z + (h - 1) + back) % NZ]
        return remote(blk, blk, dn_s.at[s, h - 1], dn_r.at[s, h - 1], dn_dev)

    def z_own(s):
        for o in range(8):
            own(s, o).wait()
        z_up(s, 1).start()
        z_dn(s, 1).start()

    z_own(0)
    z_own(1)
    z_own(2)

    for load in loads:
        load.wait()
    got[me] = send[me]

    def a2a(d, source=None):
        j = (me + d) % NDP
        source = me if source is None else source
        return remote(send.at[j], got.at[source], a2a_s.at[d - 1], a2a_r.at[d - 1], {"dp": j})

    def a2a_start(d, carry):
        a2a(d).start()
        return carry

    lax.fori_loop(1, NDP, a2a_start, 0)
    xt[...] = x_in[...].astype(jnp.float32).T.astype(jnp.bfloat16)

    mine_o = c * NX + x

    def w_x(d, back=0):
        blk = wf.at[y, c * NX + (x + NX - back) % NX]
        return remote(blk, blk, wx_s.at[d - 1], wx_r.at[d - 1], dp_at(y, (x + d) % NX, c))

    def w_y(d, back=0):
        blk = wf.at[(y + NY - back) % NY, pl.ds(c * NX, NX)]
        return remote(blk, blk, wy_s.at[d - 1], wy_r.at[d - 1], dp_at((y + d) % NY, x, c))

    def w_pair(d, cc=None):
        cc = c if cc is None else cc
        blk = wf.at[(y + NY - d) % NY, pl.ds(cc * NX, NX)]
        return remote(blk, blk, wp_s.at[d], wp_r.at[d], partner)

    def assemble():
        def arrived(d, carry):
            a2a(d, (me + NDP - d) % NDP).wait_recv()
            return carry

        lax.fori_loop(1, NDP, arrived, 0)
        units = got[...].reshape(NDP * 2 * SLOTS, 3 * UNIT)
        for e in range(2):
            wanted = wanted_rows[e : e + 1, :]
            lanes = slice(e * UNIT, (e + 1) * UNIT)
            for base in range(0, FEAT, 128):
                ids = lax.broadcasted_iota(jnp.int32, (128, NDP * 2 * SLOTS), 0) + base
                pick = jnp.where(ids == wanted, 1.0, 0.0).astype(jnp.bfloat16)
                out = jnp.dot(pick, units, preferred_element_type=jnp.float32)
                here = slice(base, base + 128)
                wf[y, mine_o, e, here, :] = out[:, :UNIT].astype(jnp.bfloat16)
                master_out[here, lanes] = out[:, :UNIT]
                moment1_out[here, lanes] = out[:, UNIT : 2 * UNIT]
                moment2_out[here, lanes] = out[:, 2 * UNIT :]
        for d in range(1, NX):
            w_x(d).start()

    def weights_y():
        for d in range(1, NX):
            w_x(d, d).wait_recv()
        for d in range(1, NY):
            w_y(d).start()
        w_pair(0).start()

    def weights_pair():
        for d in range(1, NY):
            w_y(d, d).wait_recv()
            w_pair(d).start()

    def pair(s):
        return remote(pair_s.at[s], pair_r.at[s], pr_s.at[s], pr_r.at[s], partner)

    def along_x(s, d):
        xx = (x + d) % NX
        return remote(
            xs.at[s, xx], xr.at[s, d - 1], x_s.at[s, d - 1], x_r.at[s, d - 1], dp_at(y, xx, c)
        )

    def along_y(s):
        return remote(ys.at[s], yr.at[s], y_s.at[s], y_r.at[s], dp_at(row_of(s), x, c))

    def stage_c(s):
        for d in range(1, NX):
            along_x(s, d).wait_recv()
        total = kept_x[...]
        for d in range(NX - 1):
            total += xr[s, d].astype(jnp.float32)

        @when(s < 6)
        def _():
            ys[s] = total.astype(jnp.bfloat16)
            along_y(s).start()

        @when(s == 6)
        def _():
            grad_out[:, :UNIT] = total

        @when(s == 7)
        def _():
            grad_out[:, UNIT:] = total

    def stage_b(s):
        pair(s).wait_recv()
        for d in range(1, NX):
            xx = (x + d) % NX
            lanes = pl.ds(pl.multiple_of(xx * UNIT, UNIT), UNIT)
            xs[s, xx] = (kept[:, lanes] + pair_r[s, :, lanes].astype(jnp.float32)).astype(jnp.bfloat16)
            along_x(s, d).start()
        lanes = pl.ds(pl.multiple_of(x * UNIT, UNIT), UNIT)
        kept_x[...] = kept[:, lanes] + pair_r[s, :, lanes].astype(jnp.float32)

    def stage_a(s):
        @when(s % 2 == 0)
        def _():
            z_up(s, 4, 1).wait_recv()
            z_dn(s, 3, 1).wait_recv()

        @when(s % 2 == 1)
        def _():
            z_up(s, 3, 1).wait_recv()
            z_dn(s, 4, 1).wait_recv()

        def product(half):
            parts = [g[at(s), :, half * NX + i].reshape(TOK, UNIT) for i in range(NX)]
            block = jnp.concatenate(parts, axis=1)
            return jnp.dot(xt[...], block, preferred_element_type=jnp.float32)

        pair_s[s] = product(1 - c).astype(jnp.bfloat16)
        pair(s).start()
        kept[...] = product(c)

    def input_grad(s):
        rows = jnp.concatenate([g[at(s), :, o].reshape(TOK, UNIT) for o in range(8)], axis=1)
        weights = jnp.concatenate([wf[row_of(s), o, s % 2] for o in range(8)], axis=1)
        more = lax.dot_general(
            rows, weights, (((1,), (1,)), ((), ())), preferred_element_type=jnp.float32
        )

        @when(s == 0)
        def _():
            ig[...] = more

        @when(s > 0)
        def _():
            ig[...] += more

    def wave(w, carry):
        for h in (2, 3, 4):
            s = w - (h - 1)
            up_ok = both(s >= 0, s < CHUNKS)
            dn_ok = up_ok
            if h == 4:
                up_ok, dn_ok = both(up_ok, s % 2 == 0), both(dn_ok, s % 2 == 1)

            @when(up_ok)
            def _(s=s, h=h):
                z_up(s, h - 1, 1).wait_recv()
                z_up(s, h).start()

            @when(dn_ok)
            def _(s=s, h=h):
                z_dn(s, h - 1, 1).wait_recv()
                z_dn(s, h).start()

        @when(w + 2 < CHUNKS)
        def _():
            z_own(w + 2)

        @when(both(w >= 6, w < 14))
        def _():
            stage_c(w - 6)

        @when(both(w >= 5, w < 13))
        def _():
            stage_b(w - 5)

        @when(both(w >= 4, w < 12))
        def _():
            stage_a(w - 4)

        when(w == 2)(assemble)
        when(w == 4)(weights_y)
        when(w == 7)(weights_pair)

        @when(w == 8)
        def _():
            for d in range(NY):
                w_pair(d, 1 - c).wait_recv()

        @when(both(w >= 8, w < 12))
        def _():
            input_grad(2 * (w - 8))
            input_grad(2 * (w - 8) + 1)

        return carry

    lax.fori_loop(1, 14, wave, 0)

    for e in range(2):
        lanes = slice(e * UNIT, (e + 1) * UNIT)
        total = grad_out[:, lanes]
        for k in range(NY - 1):
            along_y(2 * k + e).wait_recv()
            total += yr[2 * k + e].astype(jnp.float32)
        grad_out[:, lanes] = total

    def sent_a2a(d, carry):
        a2a(d).wait_send()
        return carry

    lax.fori_loop(1, NDP, sent_a2a, 0)

    def sent(s, carry):
        for h in (1, 2, 3):
            z_up(s, h).wait_send()
            z_dn(s, h).wait_send()

        @when(s % 2 == 0)
        def _():
            z_up(s, 4).wait_send()

        @when(s % 2 == 1)
        def _():
            z_dn(s, 4).wait_send()

        pair(s).wait_send()
        for d in range(1, NX):
            along_x(s, d).wait_send()

        @when(s < 6)
        def _():
            along_y(s).wait_send()

        return carry

    lax.fori_loop(0, CHUNKS, sent, 0)
    for d in range(1, NX):
        w_x(d).wait_send()
    for d in range(1, NY):
        w_y(d).wait_send()
    for d in range(NY):
        w_pair(d).wait_send()


def old_places(counts, owners, me):
    index = jnp.arange(NDP, dtype=jnp.int32)
    starts = jnp.sum(jnp.where(index[None, :] < index[:, None], counts[None, :], 0), axis=1)
    holds = owners[None, :] == index[:, None]
    first = jnp.sum(jnp.where(holds, starts[None, :], 0), axis=1)
    last = first + jnp.sum(jnp.where(holds, counts[None, :], 0), axis=1)
    my_start = jnp.sum(jnp.where(owners == me, starts, 0))
    lane = np.arange(NDP * 2 * SLOTS)
    column = ((lane % (2 * SLOTS)) // SLOTS).astype(np.int32)
    step = ((lane % SLOTS) * PER_ROW).astype(np.int32)
    first = jnp.broadcast_to(first[:, None], (NDP, 2 * SLOTS)).reshape(-1)
    last = jnp.broadcast_to(last[:, None], (NDP, 2 * SLOTS)).reshape(-1)
    unit = first + ((2 * me + column - first) & (PER_ROW - 1)) + step
    row = jnp.where(unit < last, unit >> 6, -1)
    return my_start, jnp.stack([jnp.where(column == e, row, -1) for e in range(2)])


def local(old_master, old_moment1, old_moment2, old_counts, old_owner, inputs, cotangent):
    bf, f32 = jnp.bfloat16, jnp.float32
    dma = pltpu.SemaphoreType.DMA
    vmem = pl.BlockSpec(memory_space=pltpu.VMEM)
    anywhere = pl.BlockSpec(memory_space=pl.ANY)
    my_start, wanted_rows = old_places(old_counts, old_owner, lax.axis_index("dp"))

    def by_column(a):
        a = a.reshape(SLOTS, PER_ROW, UNIT).transpose(1, 0, 2)
        a = lax.dynamic_slice_in_dim(
            jnp.concatenate([a, a], axis=0), (-my_start) & (PER_ROW - 1), PER_ROW, axis=0
        )
        return a.reshape(NDP, 2 * SLOTS, UNIT)

    packed = jnp.concatenate(
        [by_column(a) for a in (old_master, old_moment1, old_moment2)], axis=2
    ).astype(bf)
    owned = jax.ShapeDtypeStruct((FEAT, 2 * UNIT), f32)
    grad, master, moment1, moment2, input_grad = pl.pallas_call(
        kernel,
        out_shape=(owned, owned, owned, owned, jax.ShapeDtypeStruct((TOK, FEAT), f32)),
        in_specs=[vmem] + [anywhere] * 3,
        out_specs=[vmem] * 5,
        scratch_shapes=[
            pltpu.VMEM((TOK, FEAT), bf),
            pltpu.VMEM((FEAT, TOK), bf),
            pltpu.VMEM((CHUNKS, NZ, NC * NX, OWN, UNIT), bf),
            pltpu.VMEM((NY, NC * NX, 2, FEAT, UNIT), bf),
            pltpu.VMEM((NDP, 2 * SLOTS, 3 * UNIT), bf),
            pltpu.VMEM((NDP, 2 * SLOTS, 3 * UNIT), bf),
            pltpu.VMEM((CHUNKS, FEAT, HALF_D), bf),
            pltpu.VMEM((CHUNKS, FEAT, HALF_D), bf),
            pltpu.VMEM((FEAT, HALF_D), f32),
            pltpu.VMEM((CHUNKS, NX, FEAT, UNIT), bf),
            pltpu.VMEM((CHUNKS, NX - 1, FEAT, UNIT), bf),
            pltpu.VMEM((FEAT, UNIT), f32),
            pltpu.VMEM((6, FEAT, UNIT), bf),
            pltpu.VMEM((6, FEAT, UNIT), bf),
            dma((2,)),
            dma((CHUNKS, 8)),
            dma((CHUNKS, 4)),
            dma((CHUNKS, 4)),
            dma((CHUNKS, 4)),
            dma((CHUNKS, 4)),
            dma((NDP - 1,)),
            dma((NDP - 1,)),
            dma((NX - 1,)),
            dma((NX - 1,)),
            dma((NY - 1,)),
            dma((NY - 1,)),
            dma((NY,)),
            dma((NY,)),
            dma((CHUNKS,)),
            dma((CHUNKS,)),
            dma((CHUNKS, NX - 1)),
            dma((CHUNKS, NX - 1)),
            dma((6,)),
            dma((6,)),
        ],
        compiler_params=pltpu.CompilerParams(
            collective_id=0, has_side_effects=True, vmem_limit_bytes=62 * 1024 * 1024
        ),
        name="relay_backward",
    )(wanted_rows, packed, inputs, cotangent)
    new_moment1 = beta_one * moment1 + (1.0 - beta_one) * grad
    new_moment2 = beta_two * moment2 + (1.0 - beta_two) * grad * grad
    new_master = master - learn_rate * (
        new_moment1 / (jnp.sqrt(new_moment2) + epsilon) + weight_decay * master
    )
    return (new_master, new_moment1, new_moment2, input_grad.astype(bf))


def solution(mesh):
    placed = (
        P("tensor", "dp", None, None),
        P("tensor", "dp", None, None),
        P("tensor", "dp", None, None),
        P(),
        P(),
        P("dp", "tensor"),
        P(("dp", "tensor"), None),
    )
    return jax.shard_map(
        local,
        mesh=mesh,
        in_specs=placed,
        out_specs=(P("tensor", "dp"), P("tensor", "dp"), P("tensor", "dp"), P("dp", "tensor")),
        check_vma=False,
    )
```
